128 devices in a mesh: chan: 16 (over y_lo, z, core), tile: 8 (over y_hi, x).
Axes of the slice: x: 4, y: 4 (y_hi: 2, y_lo: 2; y = y_hi * 2 + y_lo), z: 4, core: 2. Of those that a mesh axis runs over, the one named last changes fastest.
Arguments:
- voltages: bfloat16 [524288, 2048], P('chan', 'tile'), may hold values from -4 to 4
- pfb_taps: float32 [4, 2048], replicated, may hold values from -3 to 3
Outputs:
- visibility: float32 [32, 2, 2048, 2048], P('chan', None, 'tile')
The draws below stay inside these ranges and needn't reach their ends.
All inputs are finite; a program needn't handle non-finite values.
Results may differ from the reference program's by a relative error of at most 0.0038.
Values may be sent and summed in bfloat16 or wider, within the bound.
A program may use at most 192 MiB of HBM per device.

```python
import math
import jax
import jax.numpy as jnp
from jax import lax

INPUTS = 2048
FFT_LEN = 2048
TAPS = 4
CHANNELS = 32
SPECTRA = 256
TIME = 524288


def block_levels(stream_key, extent, pieces, least, high):
    def one(axis_at, parts):
        heights = jax.random.uniform(jax.random.fold_in(jax.random.fold_in(stream_key, 6), axis_at), (parts,), jnp.float32, least / len(pieces), high / len(pieces))
        return jnp.repeat(jnp.exp(heights), extent[axis_at] // parts).reshape((-1,) + (1,) * (len(extent) - axis_at - 1))

    gain = one(*pieces[0])
    for cut in pieces[1:]:
        gain = gain * one(*cut)
    return gain


def normal_values(stream_key, dims, spread, most, cuts=(), kind=jnp.bfloat16):
    values = spread * jax.random.normal(stream_key, dims, jnp.float32)
    if cuts:
        values = values * block_levels(stream_key, dims, cuts, -0.22, 0.18)
    return jnp.clip(values, -most, most).astype(kind)


def setup_inputs(seed: int = 0) -> dict:
    key_list = jax.random.split(jax.random.key(seed), 3)
    voltages = normal_values(key_list[0], (TIME, INPUTS), 1.0, 4.0, ((0, 16), (1, 8)))
    pfb_taps = normal_values(key_list[1], (TAPS, FFT_LEN), 0.5, 3.0, (), jnp.float32)
    return {"voltages": voltages, "pfb_taps": pfb_taps}


def dft_table(frame_len, channel_count):
    samples = jnp.arange(frame_len, dtype=jnp.int32)
    centers = frame_len // 8 + jnp.arange(channel_count, dtype=jnp.int32)
    phase_index = samples[:, None] * centers[None, :] % frame_len
    angle = 2.0 * jnp.pi / frame_len * phase_index.astype(jnp.float32)
    factor = 1.0 / math.sqrt(frame_len)
    return jnp.concatenate([jnp.cos(angle) * factor, -jnp.sin(angle) * factor], axis=1)

def reference(voltages, pfb_taps):
    table = dft_table(FFT_LEN, CHANNELS)
    padded = jnp.concatenate([voltages, jnp.zeros(((TAPS - 1) * FFT_LEN, INPUTS), voltages.dtype)], axis=0)

    def one_spectrum(spec_index):
        samples = lax.dynamic_slice_in_dim(padded, spec_index * FFT_LEN, TAPS * FFT_LEN, 0)
        window = samples.astype(jnp.float32).reshape(TAPS, FFT_LEN, INPUTS)
        filtered = lax.optimization_barrier(jnp.sum(pfb_taps[:, :, None] * window, axis=0))
        return jnp.dot(table.T, filtered, precision=lax.Precision.HIGHEST, preferred_element_type=jnp.float32)
    spectra = lax.map(one_spectrum, jnp.arange(SPECTRA, dtype=jnp.int32))
    spectra = spectra.astype(jnp.bfloat16).reshape(SPECTRA, 2, CHANNELS, INPUTS)
    by_channel = jnp.transpose(spectra, (2, 0, 1, 3))

    def one_channel(samples):
        values = samples.astype(jnp.float32)
        products = jnp.einsum('sai,sbk->aibk', values, values, precision=lax.Precision.HIGHEST)
        real_part = products[0, :, 0, :] + products[1, :, 1, :]
        imag_part = products[1, :, 0, :] - products[0, :, 1, :]
        return jnp.stack([real_part, imag_part], axis=0) / SPECTRA
    return lax.map(one_channel, by_channel)
```

```python
import functools
import math

import jax
import jax.numpy as jnp
import numpy as np
from jax import lax
from jax.experimental import pallas as pl
from jax.experimental.pallas import tpu as pltpu
from jax.sharding import PartitionSpec as P

FFT = 2048
TAPS = 4
CHANNELS = 32
ROWS = 2 * CHANNELS
HALO = TAPS - 1


def dft_rows():
    samples = np.arange(FFT, dtype=np.int64)
    centers = FFT // 8 + np.arange(CHANNELS, dtype=np.int64)
    angle = 2.0 * np.pi / FFT * (centers[:, None] * samples[None, :] % FFT)
    factor = 1.0 / math.sqrt(FFT)
    return np.concatenate([np.cos(angle), -np.sin(angle)], axis=0).astype(np.float32) * np.float32(factor)


def channelize_kernel(taps_ref, table_ref, frame_ref, done_ref, tail_ref, head_ref, weights, sums):
    f = pl.program_id(0)
    last = pl.num_programs(0) - 1

    @pl.when(f == 0)
    def _():
        for t in range(TAPS):
            full = taps_ref[t : t + 1, :] * table_ref[...]
            high = full.astype(jnp.bfloat16)
            weights[2 * t * ROWS : (2 * t + 1) * ROWS, :] = high
            weights[(2 * t + 1) * ROWS : (2 * t + 2) * ROWS, :] = (full - high.astype(jnp.float32)).astype(jnp.bfloat16)
        sums[0 : HALO * ROWS, :] = jnp.zeros((HALO * ROWS, sums.shape[1]), jnp.float32)

    part = jnp.dot(weights[...], frame_ref[...], preferred_element_type=jnp.float32)
    for t in range(TAPS):
        term = part[2 * t * ROWS : (2 * t + 1) * ROWS] + part[(2 * t + 1) * ROWS : (2 * t + 2) * ROWS]
        at = pl.ds(pl.multiple_of((f + HALO - t) * ROWS, ROWS), ROWS)
        if t == 0:
            sums[at, :] = term
        else:
            sums[at, :] += term

    @pl.when(f == last)
    def _():
        count = pl.num_programs(0)
        head_ref[...] = sums[0 : HALO * ROWS, :]
        tail_ref[...] = sums[16 * ROWS : 19 * ROWS, :]
        done_ref[...] = sums[HALO * ROWS : 16 * ROWS, :].astype(jnp.bfloat16)


def channelize(pfb_taps, voltages):
    inputs = voltages.shape[1]
    frames = voltages.shape[0] // FFT
    full = lambda shape: pl.BlockSpec(shape, lambda f: (0, 0))
    return pl.pallas_call(
        channelize_kernel,
        grid=(frames,),
        in_specs=[full((TAPS, FFT)), full((ROWS, FFT)), pl.BlockSpec((FFT, inputs), lambda f: (f, 0))],
        out_specs=[full(((frames - HALO) * ROWS, inputs)), full((HALO * ROWS, inputs)), full((HALO * ROWS, inputs))],
        out_shape=[
            jax.ShapeDtypeStruct(((frames - HALO) * ROWS, inputs), jnp.bfloat16),
            jax.ShapeDtypeStruct((HALO * ROWS, inputs), jnp.float32),
            jax.ShapeDtypeStruct((HALO * ROWS, inputs), jnp.float32),
        ],
        scratch_shapes=[
            pltpu.VMEM((2 * TAPS * ROWS, FFT), jnp.bfloat16),
            pltpu.VMEM(((frames + HALO) * ROWS, inputs), jnp.float32),
        ],
        compiler_params=pltpu.CompilerParams(vmem_limit_bytes=40 << 20),
    )(pfb_taps, dft_rows(), voltages)


def correlate_kernel(scale, own_ref, other_ref, out_ref, left):
    half = own_ref.shape[1] // 2

    @pl.when(pl.program_id(1) == 0)
    def _():
        own = own_ref[0].astype(jnp.float32).T
        left[0:256, :] = own.astype(jnp.bfloat16)
        left[256:512, :] = jnp.concatenate([own[:, half:], -own[:, :half]], axis=1).astype(jnp.bfloat16)

    for q in range(other_ref.shape[0]):
        block = jnp.dot(left[...], other_ref[q, 0], preferred_element_type=jnp.float32) * scale
        out_ref[0, 0, :, q * 256 : (q + 1) * 256] = block[:256]
        out_ref[0, 1, :, q * 256 : (q + 1) * 256] = block[256:]


def correlate(own, gathered, spectra):
    tiles, channels, depth, inputs = gathered.shape
    step = 2
    return pl.pallas_call(
        functools.partial(correlate_kernel, 1.0 / spectra),
        grid=(channels, tiles // step),
        in_specs=[
            pl.BlockSpec((1, depth, inputs), lambda c, q: (c, 0, 0)),
            pl.BlockSpec((step, 1, depth, inputs), lambda c, q: (q, c, 0, 0)),
        ],
        out_specs=pl.BlockSpec((1, 2, inputs, step * inputs), lambda c, q: (c, 0, 0, q)),
        out_shape=jax.ShapeDtypeStruct((channels, 2, inputs, tiles * inputs), jnp.float32),
        scratch_shapes=[pltpu.VMEM((2 * inputs, depth), jnp.bfloat16)],
        compiler_params=pltpu.CompilerParams(vmem_limit_bytes=40 << 20),
    )(own, gathered)


def shards(voltages, pfb_taps):
    chans = lax.axis_size("chan")
    frames = voltages.shape[0] // FFT
    inputs = voltages.shape[1]
    done, tail, head = channelize(pfb_taps, voltages)
    arrived = lax.ppermute(head, "chan", [(i + 1, i) for i in range(chans - 1)])
    ending = (tail + arrived).astype(jnp.bfloat16)
    spectra = jnp.concatenate([done, ending], axis=0).reshape(frames, 2, chans, CHANNELS // chans, inputs)
    spectra = spectra.transpose(2, 3, 1, 0, 4)
    turned = lax.all_to_all(spectra, "chan", split_axis=0, concat_axis=0, tiled=True)
    own = turned.transpose(1, 2, 0, 3, 4).reshape(CHANNELS // chans, 2 * chans * frames, inputs)
    gathered = lax.all_gather(own, "tile", axis=0, tiled=False)
    return correlate(own, gathered, chans * frames)


def solution(mesh):
    placed = (P("chan", "tile"), P())
    return jax.shard_map(
        shards, mesh=mesh, in_specs=placed, out_specs=P("chan", None, "tile", None), check_vma=False
    )
```

```python
import functools
import math

import jax
import jax.numpy as jnp
import numpy as np
from jax import lax
from jax.experimental import pallas as pl
from jax.experimental.pallas import tpu as pltpu
from jax.sharding import PartitionSpec as P

MESH = pl.DeviceIdType.MESH
FFT = 2048
TAPS = 4
CHANNELS = 32
ROWS = 2 * CHANNELS
HALO = TAPS - 1
CHANS = 16
TILES = 8
RING = 4
FRAMES = 16
HALVES = 2
SPECTRA = FRAMES // HALVES
CH_DEV = CHANNELS // CHANS
INPUTS = 256
LANES = 128
PIECES = HALVES * CHANS
CUT = 9
CUT_A = 5
CUT_B = 12


def dft_rows():
    samples = np.arange(FFT, dtype=np.int64)
    centers = FFT // 8 + np.arange(CHANNELS, dtype=np.int64)
    angle = 2.0 * np.pi / FFT * (centers[:, None] * samples[None, :] % FFT)
    factor = 1.0 / math.sqrt(FFT)
    return np.concatenate([np.cos(angle), -np.sin(angle)], axis=0).astype(np.float32) * np.float32(factor)


def spread_kernel(
    taps_ref,
    table_ref,
    volt_ref,
    spread_ref,
    left_ref,
    frames,
    weights,
    sums,
    ahead,
    outbox,
    own,
    frame_sem,
    halo_send,
    halo_recv,
    turn_send,
    turn_recv,
    self_sem,
    ring_send,
    ring_recv,
    own_sem,
):
    chan = lax.axis_index("chan")
    tile = lax.axis_index("tile")
    row = tile // RING
    col = lax.rem(tile, RING)
    right = row * RING + lax.rem(col + 1, RING)
    left = row * RING + lax.rem(col + 3, RING)
    far = row * RING + lax.rem(col + 2, RING)
    other = (1 - row) * RING
    across = other + col
    across_right = other + lax.rem(col + 1, RING)
    across_left = other + lax.rem(col + 3, RING)
    across_far = other + lax.rem(col + 2, RING)

    def frame_copy(f):
        return pltpu.make_async_copy(volt_ref.at[pl.ds(f * FFT, FFT)], frames.at[f], frame_sem.at[f])

    @pl.loop(0, FRAMES)
    def _(f):
        frame_copy(f).start()

    barrier = pltpu.get_barrier_semaphore()

    @pl.loop(1, CHANS)
    def _(j):
        pl.semaphore_signal(barrier, inc=1, device_id=(lax.rem(chan + j, CHANS), tile), device_id_type=MESH)

    for peer in (right, left, across):
        pl.semaphore_signal(barrier, inc=1, device_id=(chan, peer), device_id_type=MESH)

    for t in range(TAPS):
        full = taps_ref[t : t + 1, :] * table_ref[...]
        high = full.astype(jnp.bfloat16)
        weights[2 * t * ROWS : (2 * t + 1) * ROWS, :] = high
        weights[(2 * t + 1) * ROWS : (2 * t + 2) * ROWS, :] = (full - high.astype(jnp.float32)).astype(jnp.bfloat16)
    sums[:, 0 : HALO * ROWS, :] = jnp.zeros((INPUTS // LANES, HALO * ROWS, LANES), jnp.float32)

    def channelize(start, stop):
        @pl.loop(start, stop)
        def _(f):
            frame_copy(f).wait()
            part = jnp.dot(weights[...], frames[f], preferred_element_type=jnp.float32)
            for t in range(TAPS):
                term = part[2 * t * ROWS : (2 * t + 1) * ROWS] + part[(2 * t + 1) * ROWS : (2 * t + 2) * ROWS]
                at = pl.ds(pl.multiple_of((f + HALO - t) * ROWS, ROWS), ROWS)
                for lane in range(INPUTS // LANES):
                    here = term[:, lane * LANES : (lane + 1) * LANES]
                    if t == 0:
                        sums[lane, at, :] = here
                    else:
                        sums[lane, at, :] += here

    def turn(h, j):
        peer = lax.rem(chan + j, CHANS)
        return pltpu.make_async_remote_copy(
            src_ref=outbox.at[h, peer],
            dst_ref=spread_ref.at[tile, h * CHANS + chan],
            send_sem=turn_send.at[h, peer],
            recv_sem=turn_recv.at[h, chan],
            device_id=(peer, tile),
            device_id_type=MESH,
        )

    def turned(h, j):
        peer = lax.rem(chan + j, CHANS)
        return pltpu.make_async_remote_copy(
            src_ref=outbox.at[h, peer],
            dst_ref=spread_ref.at[tile, h * CHANS + peer],
            send_sem=turn_send.at[h, peer],
            recv_sem=turn_recv.at[h, peer],
            device_id=(peer, tile),
            device_id_type=MESH,
        )

    def kept(h):
        return pltpu.make_async_copy(
            outbox.at[h, chan], spread_ref.at[tile, h * CHANS + chan], self_sem.at[h]
        )

    def send_turn(h):
        first = HALO + h * SPECTRA

        @pl.loop(0, CHANS)
        def _(p):
            for c in range(CH_DEV):
                base = first * ROWS + p * CH_DEV + c
                for lane in range(INPUTS // LANES):
                    real = sums[lane, pl.ds(base, SPECTRA, stride=ROWS), :]
                    imag = sums[lane, pl.ds(base + CHANNELS, SPECTRA, stride=ROWS), :]
                    both = jnp.concatenate([real, imag], axis=0).astype(jnp.bfloat16)
                    outbox[h, p, c, :, lane * LANES : (lane + 1) * LANES] = both

        @pl.loop(1, CHANS)
        def _(j):
            turn(h, j).start()

        kept(h).start()

    def wait_turn(h):
        @pl.loop(1, CHANS)
        def _(j):
            turned(h, j).wait_recv()

        kept(h).wait()

    def piece(h, start, stop):
        return pl.ds(h * CHANS + start, stop - start)

    part_a, part_b = (0, CUT), (CUT, CHANS)
    a_one, a_two = (0, CUT_A), (CUT_A, CUT)
    b_one, b_two = (CUT, CUT_B), (CUT_B, CHANS)
    kinds = (
        (right, tile, left, part_a),
        (right, tile, left, part_b),
        (right, across, across_left, part_a),
        (right, left, far, a_one),
        (right, left, far, b_one),
        (right, across_left, across_far, a_one),
        (left, tile, right, part_a),
        (left, tile, right, part_b),
        (left, across, across_right, part_a),
        (left, right, far, a_two),
        (left, right, far, b_two),
        (left, across_right, across_far, a_two),
        (across, tile, across, part_a),
        (across, tile, across, part_b),
        (across, left, across_left, part_b),
        (across, right, across_right, part_b),
        (across, far, across_far, b_one),
        (across, far, across_far, b_two),
    )

    def message(h, kind, arriving):
        to, sent, received, pieces = kinds[kind]
        slot = received if arriving else sent
        block = spread_ref.at[slot, piece(h, *pieces)]
        return pltpu.make_async_remote_copy(
            src_ref=block,
            dst_ref=block,
            send_sem=ring_send.at[h, kind],
            recv_sem=ring_recv.at[h, kind],
            device_id=(chan, to),
            device_id_type=MESH,
        )

    def send(h, *which):
        for kind in which:
            message(h, kind, False).start()

    def wait(h, *which):
        for kind in which:
            message(h, kind, True).wait_recv()

    def open_ring(h):
        wait_turn(h)
        send(h, 12, 0, 6, 1, 7, 13)

    def first_hops(h):
        wait(h, 12)
        send(h, 2, 8)
        wait(h, 1)
        send(h, 4, 14)
        wait(h, 7)
        send(h, 10, 15)

    def last_hops(h):
        wait(h, 0)
        send(h, 3)
        wait(h, 6)
        send(h, 9)
        wait(h, 4)
        send(h, 16)
        wait(h, 10)
        send(h, 17)
        wait(h, 2)
        send(h, 5)
        wait(h, 8)
        send(h, 11)

    channelize(0, HALO)
    pl.semaphore_wait(barrier, CHANS - 1 + 3)
    behind = pltpu.make_async_remote_copy(
        src_ref=sums.at[:, pl.ds(0, HALO * ROWS)],
        dst_ref=ahead,
        send_sem=halo_send,
        recv_sem=halo_recv,
        device_id=(lax.rem(chan + CHANS - 1, CHANS), tile),
        device_id_type=MESH,
    )
    behind.start()
    channelize(HALO, SPECTRA + HALO)
    send_turn(0)
    channelize(SPECTRA + HALO, FRAMES)
    behind.wait()
    ending = pl.ds(FRAMES * ROWS, HALO * ROWS)
    sums[:, ending, :] += jnp.where(chan == CHANS - 1, 0.0, ahead[...])
    send_turn(1)
    open_ring(0)
    first_hops(0)
    open_ring(1)
    fetch = pltpu.make_async_copy(spread_ref.at[tile], own, own_sem)
    fetch.start()
    last_hops(0)
    first_hops(1)
    last_hops(1)
    fetch.wait()
    for c in range(CH_DEV):
        mine = own[:, c].astype(jnp.float32).reshape(PIECES, 2, SPECTRA, INPUTS)
        swapped = jnp.stack([mine[:, 1], -mine[:, 0]], axis=1)
        depth = PIECES * 2 * SPECTRA
        left_ref[c, 0:INPUTS, :] = mine.reshape(depth, INPUTS).T.astype(jnp.bfloat16)
        left_ref[c, INPUTS : 2 * INPUTS, :] = swapped.reshape(depth, INPUTS).T.astype(jnp.bfloat16)
    for h in range(HALVES):
        wait(h, 3, 9, 5, 11, 13, 14, 15, 16, 17)
    for h in range(HALVES):
        for kind in range(len(kinds)):
            message(h, kind, False).wait_send()

        @pl.loop(1, CHANS)
        def _(j):
            turn(h, j).wait_send()


def spread(pfb_taps, voltages):
    kinds = 18
    depth = PIECES * 2 * SPECTRA
    vmem = pl.BlockSpec(memory_space=pltpu.VMEM)
    hbm = pl.BlockSpec(memory_space=pl.ANY)
    dma = pltpu.SemaphoreType.DMA
    return pl.pallas_call(
        spread_kernel,
        in_specs=[vmem, vmem, hbm],
        out_specs=[hbm, vmem],
        out_shape=[
            jax.ShapeDtypeStruct((TILES, PIECES, CH_DEV, 2 * SPECTRA, INPUTS), jnp.bfloat16),
            jax.ShapeDtypeStruct((CH_DEV, 2 * INPUTS, depth), jnp.bfloat16),
        ],
        scratch_shapes=[
            pltpu.VMEM((FRAMES, FFT, INPUTS), jnp.bfloat16),
            pltpu.VMEM((2 * TAPS * ROWS, FFT), jnp.bfloat16),
            pltpu.VMEM((INPUTS // LANES, (FRAMES + HALO) * ROWS, LANES), jnp.float32),
            pltpu.VMEM((INPUTS // LANES, HALO * ROWS, LANES), jnp.float32),
            pltpu.VMEM((HALVES, CHANS, CH_DEV, 2 * SPECTRA, INPUTS), jnp.bfloat16),
            pltpu.VMEM((PIECES, CH_DEV, 2 * SPECTRA, INPUTS), jnp.bfloat16),
            dma((FRAMES,)),
            dma,
            dma,
            dma((HALVES, CHANS)),
            dma((HALVES, CHANS)),
            dma((HALVES,)),
            dma((HALVES, kinds)),
            dma((HALVES, kinds)),
            dma,
        ],
        compiler_params=pltpu.CompilerParams(
            collective_id=0, has_side_effects=True, vmem_limit_bytes=48 << 20
        ),
    )(pfb_taps, dft_rows(), voltages)


def correlate_kernel(scale, left_ref, other_ref, out_ref):
    for q in range(other_ref.shape[0]):
        right = other_ref[q, :, 0].reshape(left_ref.shape[2], INPUTS)
        block = jnp.dot(left_ref[0], right, preferred_element_type=jnp.float32) * scale
        out_ref[0, 0, :, q * INPUTS : (q + 1) * INPUTS] = block[:INPUTS]
        out_ref[0, 1, :, q * INPUTS : (q + 1) * INPUTS] = block[INPUTS:]


def correlate(left, gathered):
    depth = left.shape[2]
    step = 2
    return pl.pallas_call(
        functools.partial(correlate_kernel, 1.0 / (CHANS * FRAMES)),
        grid=(CH_DEV, TILES // step),
        in_specs=[
            pl.BlockSpec((1, 2 * INPUTS, depth), lambda c, q: (c, 0, 0)),
            pl.BlockSpec((step, PIECES, 1, 2 * SPECTRA, INPUTS), lambda c, q: (q, 0, c, 0, 0)),
        ],
        out_specs=pl.BlockSpec((1, 2, INPUTS, step * INPUTS), lambda c, q: (c, 0, 0, q)),
        out_shape=jax.ShapeDtypeStruct((CH_DEV, 2, INPUTS, TILES * INPUTS), jnp.float32),
        compiler_params=pltpu.CompilerParams(vmem_limit_bytes=32 << 20),
    )(left, gathered)


def shards(voltages, pfb_taps):
    gathered, left = spread(pfb_taps, voltages)
    return correlate(left, gathered)


def solution(mesh):
    placed = (P("chan", "tile"), P())
    return jax.shard_map(
        shards, mesh=mesh, in_specs=placed, out_specs=P("chan", None, "tile", None), check_vma=False
    )
```

```python
import functools
import math

import jax
import jax.numpy as jnp
import numpy as np
from jax import lax
from jax.experimental import pallas as pl
from jax.experimental.pallas import tpu as pltpu
from jax.sharding import PartitionSpec as P

MESH = pl.DeviceIdType.MESH
FFT = 2048
TAPS = 4
CHANNELS = 32
ROWS = 2 * CHANNELS
HALO = TAPS - 1
CHANS = 16
TILES = 8
RING = 4
FRAMES = 16
PARTS = 4
SPECTRA = FRAMES // PARTS
BLOCK = 2 * SPECTRA
CHUNKS = ((0, 2), (2, 4))
PAUSE = 16
STEP = 2
CH_DEV = CHANNELS // CHANS
INPUTS = 256
LANES = 128
DEPTH = 2 * FRAMES * CHANS
CUT = 9
CUT_A = 5
CUT_B = 12


def dft_rows():
    samples = np.arange(FFT, dtype=np.int64)
    centers = FFT // 8 + np.arange(CHANNELS, dtype=np.int64)
    angle = 2.0 * np.pi / FFT * (centers[:, None] * samples[None, :] % FFT)
    factor = 1.0 / math.sqrt(FFT)
    return np.concatenate([np.cos(angle), -np.sin(angle)], axis=0).astype(np.float32) * np.float32(factor)


def folded(pfb_taps):
    full = pfb_taps[:, None, :] * dft_rows()[None]
    high = lax.reduce_precision(full, 8, 7)
    shape = (TAPS * ROWS, FFT)
    return high.astype(jnp.bfloat16).reshape(shape), (full - high).astype(jnp.bfloat16).reshape(shape)


def spread_kernel(
    high_ref,
    low_ref,
    volt_ref,
    spread_ref,
    left_ref,
    frames,
    weights,
    sums,
    ahead,
    outbox,
    own,
    frame_sem,
    halo_send,
    halo_recv,
    turn_send,
    turn_recv,
    self_sem,
    ring_send,
    ring_recv,
    own_sem,
):
    chan = lax.axis_index("chan")
    tile = lax.axis_index("tile")
    row = tile // RING
    col = lax.rem(tile, RING)
    right = row * RING + lax.rem(col + 1, RING)
    left = row * RING + lax.rem(col + 3, RING)
    far = row * RING + lax.rem(col + 2, RING)
    other = (1 - row) * RING
    across = other + col
    across_right = other + lax.rem(col + 1, RING)
    across_left = other + lax.rem(col + 3, RING)
    across_far = other + lax.rem(col + 2, RING)

    def frame_copy(f):
        return pltpu.make_async_copy(volt_ref.at[pl.ds(f * FFT, FFT)], frames.at[f], frame_sem.at[f])

    @pl.loop(0, FRAMES)
    def _(f):
        frame_copy(f).start()

    barrier = pltpu.get_barrier_semaphore()

    @pl.loop(1, CHANS)
    def _(j):
        pl.semaphore_signal(barrier, inc=1, device_id=(lax.rem(chan + j, CHANS), tile), device_id_type=MESH)

    for peer in (right, left, across):
        pl.semaphore_signal(barrier, inc=1, device_id=(chan, peer), device_id_type=MESH)

    weights[0 : TAPS * ROWS, :] = high_ref[...]
    weights[TAPS * ROWS :, :] = low_ref[...]
    sums[:, 0 : HALO * ROWS, :] = jnp.zeros((INPUTS // LANES, HALO * ROWS, LANES), jnp.float32)

    def channelize(start, stop):
        @pl.loop(start, stop)
        def _(f):
            frame_copy(f).wait()
            part = jnp.dot(weights[...], frames[f], preferred_element_type=jnp.float32)
            for t in range(TAPS):
                term = part[t * ROWS : (t + 1) * ROWS] + part[(TAPS + t) * ROWS : (TAPS + t + 1) * ROWS]
                at = pl.ds(pl.multiple_of((f + HALO - t) * ROWS, ROWS), ROWS)
                for lane in range(INPUTS // LANES):
                    here = term[:, lane * LANES : (lane + 1) * LANES]
                    if t == 0:
                        sums[lane, at, :] = here
                    else:
                        sums[lane, at, :] += here

    def rows(h):
        first, last = CHUNKS[h]
        return pl.ds(first * BLOCK, (last - first) * BLOCK)

    def turn(h, j, arriving):
        peer = lax.rem(chan + j, CHANS)
        return pltpu.make_async_remote_copy(
            src_ref=outbox.at[peer, :, rows(h)],
            dst_ref=spread_ref.at[tile, peer if arriving else chan, :, rows(h)],
            send_sem=turn_send.at[h, peer],
            recv_sem=turn_recv.at[h, peer if arriving else chan],
            device_id=(peer, tile),
            device_id_type=MESH,
        )

    def kept(h):
        return pltpu.make_async_copy(
            outbox.at[chan, :, rows(h)], spread_ref.at[tile, chan, :, rows(h)], self_sem.at[h]
        )

    def send_turn(h):
        @pl.loop(0, CHANS)
        def _(p):
            for c in range(CH_DEV):
                for part in range(*CHUNKS[h]):
                    base = (HALO + part * SPECTRA) * ROWS + p * CH_DEV + c
                    for lane in range(INPUTS // LANES):
                        real = sums[lane, pl.ds(base, SPECTRA, stride=ROWS), :]
                        imag = sums[lane, pl.ds(base + CHANNELS, SPECTRA, stride=ROWS), :]
                        both = jnp.concatenate([real, imag], axis=0).astype(jnp.bfloat16)
                        outbox[p, c, part * BLOCK : (part + 1) * BLOCK, lane * LANES : (lane + 1) * LANES] = both

        @pl.loop(1, CHANS)
        def _(j):
            turn(h, j, False).start()

        kept(h).start()

    def wait_turn(h):
        @pl.loop(1, CHANS)
        def _(j):
            turn(h, j, True).wait_recv()

        kept(h).wait()

    part_a, part_b = (0, CUT), (CUT, CHANS)
    a_one, a_two = (0, CUT_A), (CUT_A, CUT)
    b_one, b_two = (CUT, CUT_B), (CUT_B, CHANS)
    kinds = (
        (right, tile, left, part_a),
        (right, tile, left, part_b),
        (right, across, across_left, part_a),
        (right, left, far, a_one),
        (right, left, far, b_one),
        (right, across_left, across_far, a_one),
        (left, tile, right, part_a),
        (left, tile, right, part_b),
        (left, across, across_right, part_a),
        (left, right, far, a_two),
        (left, right, far, b_two),
        (left, across_right, across_far, a_two),
        (across, tile, across, part_a),
        (across, tile, across, part_b),
        (across, left, across_left, part_b),
        (across, right, across_right, part_b),
        (across, far, across_far, b_one),
        (across, far, across_far, b_two),
    )

    def message(h, kind, arriving):
        to, sent, received, pieces = kinds[kind]
        slot = received if arriving else sent
        block = spread_ref.at[slot, pl.ds(pieces[0], pieces[1] - pieces[0]), :, rows(h)]
        return pltpu.make_async_remote_copy(
            src_ref=block,
            dst_ref=block,
            send_sem=ring_send.at[h, kind],
            recv_sem=ring_recv.at[h, kind],
            device_id=(chan, to),
            device_id_type=MESH,
        )

    def send(h, *which):
        for kind in which:
            message(h, kind, False).start()

    def wait(h, *which):
        for kind in which:
            message(h, kind, True).wait_recv()

    def open_ring(h):
        wait_turn(h)
        send(h, 12, 0, 6, 1, 7, 13)

    def first_hops(h):
        wait(h, 12)
        send(h, 2, 8)
        wait(h, 1)
        send(h, 4, 14)
        wait(h, 7)
        send(h, 10, 15)

    def last_hops(h):
        wait(h, 0)
        send(h, 3)
        wait(h, 6)
        send(h, 9)
        wait(h, 4)
        send(h, 16)
        wait(h, 10)
        send(h, 17)
        wait(h, 2)
        send(h, 5)
        wait(h, 8)
        send(h, 11)

    channelize(0, HALO)
    pl.semaphore_wait(barrier, CHANS - 1 + 3)
    behind = pltpu.make_async_remote_copy(
        src_ref=sums.at[:, pl.ds(0, HALO * ROWS)],
        dst_ref=ahead,
        send_sem=halo_send,
        recv_sem=halo_recv,
        device_id=(lax.rem(chan + CHANS - 1, CHANS), tile),
        device_id_type=MESH,
    )
    behind.start()
    ready = [last * SPECTRA + HALO for _, last in CHUNKS[:-1]]
    channelize(HALO, ready[0])
    send_turn(0)
    channelize(ready[0], PAUSE)
    open_ring(0)
    channelize(PAUSE, FRAMES)
    behind.wait()
    ending = pl.ds(FRAMES * ROWS, HALO * ROWS)
    sums[:, ending, :] += jnp.where(chan == CHANS - 1, 0.0, ahead[...])
    send_turn(1)
    first_hops(0)
    open_ring(1)
    fetch = pltpu.make_async_copy(spread_ref.at[tile], own, own_sem)
    fetch.start()
    last_hops(0)
    fetch.wait()

    def prepare(c):
        mine = own[:, c].astype(jnp.float32).reshape(DEPTH, INPUTS).T
        at = lax.broadcasted_iota(jnp.int32, mine.shape, 1)
        upper = lax.rem(at, BLOCK) < SPECTRA
        swapped = jnp.where(upper, jnp.roll(mine, -SPECTRA, axis=1), -jnp.roll(mine, SPECTRA, axis=1))
        left_ref[c, 0:INPUTS, :] = mine.astype(jnp.bfloat16)
        left_ref[c, INPUTS : 2 * INPUTS, :] = swapped.astype(jnp.bfloat16)

    prepare(0)
    first_hops(1)
    prepare(1)
    last_hops(1)
    for h in range(len(CHUNKS)):
        wait(h, 3, 9, 5, 11, 13, 14, 15, 16, 17)
    for h in range(len(CHUNKS)):
        for kind in range(len(kinds)):
            message(h, kind, False).wait_send()

        @pl.loop(1, CHANS)
        def _(j):
            turn(h, j, False).wait_send()


def spread(high, low, voltages):
    kinds = 18
    chunks = len(CHUNKS)
    vmem = pl.BlockSpec(memory_space=pltpu.VMEM)
    hbm = pl.BlockSpec(memory_space=pltpu.HBM)
    dma = pltpu.SemaphoreType.DMA
    return pl.pallas_call(
        spread_kernel,
        in_specs=[vmem, vmem, hbm],
        out_specs=[vmem, vmem],
        out_shape=[
            jax.ShapeDtypeStruct((TILES, CHANS, CH_DEV, 2 * FRAMES, INPUTS), jnp.bfloat16),
            jax.ShapeDtypeStruct((CH_DEV, 2 * INPUTS, DEPTH), jnp.bfloat16),
        ],
        scratch_shapes=[
            pltpu.VMEM((FRAMES, FFT, INPUTS), jnp.bfloat16),
            pltpu.VMEM((2 * TAPS * ROWS, FFT), jnp.bfloat16),
            pltpu.VMEM((INPUTS // LANES, (FRAMES + HALO) * ROWS, LANES), jnp.float32),
            pltpu.VMEM((INPUTS // LANES, HALO * ROWS, LANES), jnp.float32),
            pltpu.VMEM((CHANS, CH_DEV, 2 * FRAMES, INPUTS), jnp.bfloat16),
            pltpu.VMEM((CHANS, CH_DEV, 2 * FRAMES, INPUTS), jnp.bfloat16),
            dma((FRAMES,)),
            dma,
            dma,
            dma((chunks, CHANS)),
            dma((chunks, CHANS)),
            dma((chunks,)),
            dma((chunks, kinds)),
            dma((chunks, kinds)),
            dma,
        ],
        compiler_params=pltpu.CompilerParams(
            collective_id=0, has_side_effects=True, vmem_limit_bytes=44 << 20
        ),
    )(high, low, voltages)


def correlate_kernel(scale, left_ref, other_ref, out_ref, planes, sems):
    copies = []
    for c in range(CH_DEV):
        for q in range(TILES):
            right = other_ref[q, :, c].reshape(DEPTH, INPUTS)
            block = jnp.dot(left_ref[c], right, preferred_element_type=jnp.float32) * scale
            planes[c, 0, :, q * INPUTS : (q + 1) * INPUTS] = block[:INPUTS]
            planes[c, 1, :, q * INPUTS : (q + 1) * INPUTS] = block[INPUTS:]
            if (q + 1) % STEP == 0:
                columns = pl.ds((q + 1 - STEP) * INPUTS, STEP * INPUTS)
                copies.append(
                    pltpu.make_async_copy(
                        planes.at[c, :, :, columns], out_ref.at[c, :, :, columns], sems.at[len(copies)]
                    )
                )
                copies[-1].start()
    for copy in copies:
        copy.wait()


def correlate(left, gathered):
    vmem = pl.BlockSpec(memory_space=pltpu.VMEM)
    shape = (CH_DEV, 2, INPUTS, TILES * INPUTS)
    return pl.pallas_call(
        functools.partial(correlate_kernel, 1.0 / (CHANS * FRAMES)),
        in_specs=[vmem, vmem],
        out_specs=pl.BlockSpec(memory_space=pltpu.HBM),
        out_shape=jax.ShapeDtypeStruct(shape, jnp.float32),
        scratch_shapes=[
            pltpu.VMEM(shape, jnp.float32),
            pltpu.SemaphoreType.DMA((CH_DEV * TILES // STEP,)),
        ],
        compiler_params=pltpu.CompilerParams(vmem_limit_bytes=16 << 20),
    )(left, gathered)


def shards(voltages, pfb_taps):
    gathered, left = spread(*folded(pfb_taps), voltages)
    return correlate(left, gathered)


def solution(mesh):
    placed = (P("chan", "tile"), P())
    return jax.shard_map(
        shards, mesh=mesh, in_specs=placed, out_specs=P("chan", None, "tile", None), check_vma=False
    )
```

```python
import functools
import math

import jax
import jax.numpy as jnp
import numpy as np
from jax import lax
from jax.experimental import pallas as pl
from jax.experimental.pallas import tpu as pltpu
from jax.sharding import PartitionSpec as P

MESH = pl.DeviceIdType.MESH
FFT = 2048
TAPS = 4
CHANNELS = 32
ROWS = 2 * CHANNELS
HALO = TAPS - 1
CHANS = 16
TILES = 8
RING = 4
FRAMES = 16
PARTS = 2
SPECTRA = FRAMES // PARTS
BLOCK = 2 * SPECTRA
CHUNKS = ((0, 1), (1, 2))
PAUSE = 16
STEP = 2
CH_DEV = CHANNELS // CHANS
INPUTS = 256
LANES = 128
DEPTH = 2 * FRAMES * CHANS
CUT = 9
CUT_A = 5
CUT_B = 12


def dft_rows():
    samples = np.arange(FFT, dtype=np.int64)
    centers = FFT // 8 + np.arange(CHANNELS, dtype=np.int64)
    angle = 2.0 * np.pi / FFT * (centers[:, None] * samples[None, :] % FFT)
    factor = 1.0 / math.sqrt(FFT)
    return np.concatenate([np.cos(angle), -np.sin(angle)], axis=0).astype(np.float32) * np.float32(factor)


def folded(pfb_taps):
    full = pfb_taps[:, None, :] * dft_rows()[None]
    high = lax.reduce_precision(full, 8, 7)
    shape = (TAPS * ROWS, FFT)
    return high.astype(jnp.bfloat16).reshape(shape), (full - high).astype(jnp.bfloat16).reshape(shape)


def spread_kernel(
    high_ref,
    low_ref,
    volt_ref,
    spread_ref,
    left_ref,
    frames,
    weights,
    sums,
    ahead,
    outbox,
    own,
    frame_sem,
    halo_send,
    halo_recv,
    turn_send,
    turn_recv,
    self_sem,
    ring_send,
    ring_recv,
    own_sem,
):
    chan = lax.axis_index("chan")
    tile = lax.axis_index("tile")
    row = tile // RING
    col = lax.rem(tile, RING)
    right = row * RING + lax.rem(col + 1, RING)
    left = row * RING + lax.rem(col + 3, RING)
    far = row * RING + lax.rem(col + 2, RING)
    other = (1 - row) * RING
    across = other + col
    across_right = other + lax.rem(col + 1, RING)
    across_left = other + lax.rem(col + 3, RING)
    across_far = other + lax.rem(col + 2, RING)

    def frame_copy(f):
        return pltpu.make_async_copy(volt_ref.at[pl.ds(f * FFT, FFT)], frames.at[f], frame_sem.at[f])

    @pl.loop(0, FRAMES)
    def _(f):
        frame_copy(f).start()

    barrier = pltpu.get_barrier_semaphore()

    @pl.loop(1, CHANS)
    def _(j):
        pl.semaphore_signal(barrier, inc=1, device_id=(lax.rem(chan + j, CHANS), tile), device_id_type=MESH)

    for peer in (right, left, across):
        pl.semaphore_signal(barrier, inc=1, device_id=(chan, peer), device_id_type=MESH)

    weights[0 : TAPS * ROWS, :] = high_ref[...]
    weights[TAPS * ROWS :, :] = low_ref[...]
    sums[:, 0 : HALO * ROWS, :] = jnp.zeros((INPUTS // LANES, HALO * ROWS, LANES), jnp.float32)

    def add_frame(part, f):
        for t in range(TAPS):
            term = part[t * ROWS : (t + 1) * ROWS] + part[(TAPS + t) * ROWS : (TAPS + t + 1) * ROWS]
            at = pl.ds(pl.multiple_of((f + HALO - t) * ROWS, ROWS), ROWS)
            for lane in range(INPUTS // LANES):
                here = term[:, lane * LANES : (lane + 1) * LANES]
                if t == 0:
                    sums[lane, at, :] = here
                else:
                    sums[lane, at, :] += here

    def channelize(start, stop):
        @pl.loop(0, (stop - start) // 2)
        def _(g):
            f = start + 2 * g
            frame_copy(f).wait()
            frame_copy(f + 1).wait()
            pair = jnp.concatenate([frames[f], frames[f + 1]], axis=1)
            part = jnp.dot(weights[...], pair, preferred_element_type=jnp.float32)
            add_frame(part[:, :INPUTS], f)
            add_frame(part[:, INPUTS:], f + 1)

        if (stop - start) % 2:
            frame_copy(stop - 1).wait()
            add_frame(jnp.dot(weights[...], frames[stop - 1], preferred_element_type=jnp.float32), stop - 1)

    def turn(h, j, arriving):
        peer = lax.rem(chan + j, CHANS)
        return pltpu.make_async_remote_copy(
            src_ref=outbox.at[h, peer],
            dst_ref=spread_ref.at[tile, h * CHANS + (peer if arriving else chan)],
            send_sem=turn_send.at[h, peer],
            recv_sem=turn_recv.at[h, peer if arriving else chan],
            device_id=(peer, tile),
            device_id_type=MESH,
        )

    def kept(h):
        return pltpu.make_async_copy(
            outbox.at[h, chan], spread_ref.at[tile, h * CHANS + chan], self_sem.at[h]
        )

    def send_turn(h):
        @pl.loop(0, CHANS)
        def _(p):
            for c in range(CH_DEV):
                for part in range(*CHUNKS[h]):
                    base = (HALO + part * SPECTRA) * ROWS + p * CH_DEV + c
                    for lane in range(INPUTS // LANES):
                        real = sums[lane, pl.ds(base, SPECTRA, stride=ROWS), :]
                        imag = sums[lane, pl.ds(base + CHANNELS, SPECTRA, stride=ROWS), :]
                        both = jnp.concatenate([real, imag], axis=0).astype(jnp.bfloat16)
                        outbox[part, p, c, :, lane * LANES : (lane + 1) * LANES] = both

        @pl.loop(1, CHANS)
        def _(j):
            turn(h, j, False).start()

        kept(h).start()

    def wait_turn(h):
        @pl.loop(1, CHANS)
        def _(j):
            turn(h, j, True).wait_recv()

        kept(h).wait()

    part_a, part_b = (0, CUT), (CUT, CHANS)
    a_one, a_two = (0, CUT_A), (CUT_A, CUT)
    b_one, b_two = (CUT, CUT_B), (CUT_B, CHANS)
    kinds = (
        (right, tile, left, part_a),
        (right, tile, left, part_b),
        (right, across, across_left, part_a),
        (right, left, far, a_one),
        (right, left, far, b_one),
        (right, across_left, across_far, a_one),
        (left, tile, right, part_a),
        (left, tile, right, part_b),
        (left, across, across_right, part_a),
        (left, right, far, a_two),
        (left, right, far, b_two),
        (left, across_right, across_far, a_two),
        (across, tile, across, part_a),
        (across, tile, across, part_b),
        (across, left, across_left, part_b),
        (across, right, across_right, part_b),
        (across, far, across_far, b_one),
        (across, far, across_far, b_two),
    )

    def message(h, kind, arriving):
        to, sent, received, pieces = kinds[kind]
        slot = received if arriving else sent
        block = spread_ref.at[slot, pl.ds(h * CHANS + pieces[0], pieces[1] - pieces[0])]
        return pltpu.make_async_remote_copy(
            src_ref=block,
            dst_ref=block,
            send_sem=ring_send.at[h, kind],
            recv_sem=ring_recv.at[h, kind],
            device_id=(chan, to),
            device_id_type=MESH,
        )

    def send(h, *which):
        for kind in which:
            message(h, kind, False).start()

    def wait(h, *which):
        for kind in which:
            message(h, kind, True).wait_recv()

    def open_ring(h):
        wait_turn(h)
        send(h, 12, 1, 7, 0, 6, 13)

    def first_hops(h):
        wait(h, 12)
        send(h, 2, 8)
        wait(h, 1)
        send(h, 4, 14)
        wait(h, 7)
        send(h, 10, 15)

    def last_hops(h):
        wait(h, 0)
        send(h, 3)
        wait(h, 6)
        send(h, 9)
        wait(h, 4)
        send(h, 16)
        wait(h, 10)
        send(h, 17)
        wait(h, 2)
        send(h, 5)
        wait(h, 8)
        send(h, 11)

    channelize(0, HALO + 1)
    pl.semaphore_wait(barrier, CHANS - 1 + 3)
    behind = pltpu.make_async_remote_copy(
        src_ref=sums.at[:, pl.ds(0, HALO * ROWS)],
        dst_ref=ahead,
        send_sem=halo_send,
        recv_sem=halo_recv,
        device_id=(lax.rem(chan + CHANS - 1, CHANS), tile),
        device_id_type=MESH,
    )
    behind.start()
    ready = [last * SPECTRA + HALO for _, last in CHUNKS[:-1]]
    channelize(HALO + 1, ready[0])
    send_turn(0)
    channelize(ready[0], PAUSE)
    open_ring(0)
    channelize(PAUSE, FRAMES)
    behind.wait()
    ending = pl.ds(FRAMES * ROWS, HALO * ROWS)
    sums[:, ending, :] += jnp.where(chan == CHANS - 1, 0.0, ahead[...])
    send_turn(1)
    first_hops(0)
    open_ring(1)
    fetch = pltpu.make_async_copy(spread_ref.at[tile], own, own_sem)
    fetch.start()
    last_hops(0)
    fetch.wait()

    def prepare(c):
        mine = own[:, c].astype(jnp.float32).reshape(DEPTH, INPUTS).T
        at = lax.broadcasted_iota(jnp.int32, mine.shape, 1)
        upper = lax.rem(at, BLOCK) < SPECTRA
        swapped = jnp.where(upper, jnp.roll(mine, -SPECTRA, axis=1), -jnp.roll(mine, SPECTRA, axis=1))
        left_ref[c, 0:INPUTS, :] = mine.astype(jnp.bfloat16)
        left_ref[c, INPUTS : 2 * INPUTS, :] = swapped.astype(jnp.bfloat16)

    prepare(0)
    first_hops(1)
    prepare(1)
    last_hops(1)
    for h in range(len(CHUNKS)):
        wait(h, 3, 9, 5, 11, 13, 14, 15, 16, 17)
    for h in range(len(CHUNKS)):
        for kind in range(len(kinds)):
            message(h, kind, False).wait_send()

        @pl.loop(1, CHANS)
        def _(j):
            turn(h, j, False).wait_send()


def spread(high, low, voltages):
    kinds = 18
    chunks = len(CHUNKS)
    vmem = pl.BlockSpec(memory_space=pltpu.VMEM)
    hbm = pl.BlockSpec(memory_space=pltpu.HBM)
    dma = pltpu.SemaphoreType.DMA
    return pl.pallas_call(
        spread_kernel,
        in_specs=[vmem, vmem, hbm],
        out_specs=[vmem, vmem],
        out_shape=[
            jax.ShapeDtypeStruct((TILES, PARTS * CHANS, CH_DEV, BLOCK, INPUTS), jnp.bfloat16),
            jax.ShapeDtypeStruct((CH_DEV, 2 * INPUTS, DEPTH), jnp.bfloat16),
        ],
        scratch_shapes=[
            pltpu.VMEM((FRAMES, FFT, INPUTS), jnp.bfloat16),
            pltpu.VMEM((2 * TAPS * ROWS, FFT), jnp.bfloat16),
            pltpu.VMEM((INPUTS // LANES, (FRAMES + HALO) * ROWS, LANES), jnp.float32),
            pltpu.VMEM((INPUTS // LANES, HALO * ROWS, LANES), jnp.float32),
            pltpu.VMEM((PARTS, CHANS, CH_DEV, BLOCK, INPUTS), jnp.bfloat16),
            pltpu.VMEM((PARTS * CHANS, CH_DEV, BLOCK, INPUTS), jnp.bfloat16),
            dma((FRAMES,)),
            dma,
            dma,
            dma((chunks, CHANS)),
            dma((chunks, CHANS)),
            dma((chunks,)),
            dma((chunks, kinds)),
            dma((chunks, kinds)),
            dma,
        ],
        compiler_params=pltpu.CompilerParams(
            collective_id=0, has_side_effects=True, vmem_limit_bytes=44 << 20
        ),
    )(high, low, voltages)


def correlate_kernel(scale, left_ref, other_ref, out_ref, planes, sems):
    copies = []
    for c in range(CH_DEV):
        for q in range(TILES):
            right = other_ref[q, :, c].reshape(DEPTH, INPUTS)
            block = jnp.dot(left_ref[c], right, preferred_element_type=jnp.float32) * scale
            planes[c, 0, :, q * INPUTS : (q + 1) * INPUTS] = block[:INPUTS]
            planes[c, 1, :, q * INPUTS : (q + 1) * INPUTS] = block[INPUTS:]
            if (q + 1) % STEP == 0:
                columns = pl.ds((q + 1 - STEP) * INPUTS, STEP * INPUTS)
                copies.append(
                    pltpu.make_async_copy(
                        planes.at[c, :, :, columns], out_ref.at[c, :, :, columns], sems.at[len(copies)]
                    )
                )
                copies[-1].start()
    for copy in copies:
        copy.wait()


def correlate(left, gathered):
    vmem = pl.BlockSpec(memory_space=pltpu.VMEM)
    shape = (CH_DEV, 2, INPUTS, TILES * INPUTS)
    return pl.pallas_call(
        functools.partial(correlate_kernel, 1.0 / (CHANS * FRAMES)),
        in_specs=[vmem, vmem],
        out_specs=pl.BlockSpec(memory_space=pltpu.HBM),
        out_shape=jax.ShapeDtypeStruct(shape, jnp.float32),
        scratch_shapes=[
            pltpu.VMEM(shape, jnp.float32),
            pltpu.SemaphoreType.DMA((CH_DEV * TILES // STEP,)),
        ],
        compiler_params=pltpu.CompilerParams(vmem_limit_bytes=16 << 20),
    )(left, gathered)


def shards(voltages, pfb_taps):
    gathered, left = spread(*folded(pfb_taps), voltages)
    return correlate(left, gathered)


def solution(mesh):
    placed = (P("chan", "tile"), P())
    return jax.shard_map(
        shards, mesh=mesh, in_specs=placed, out_specs=P("chan", None, "tile", None), check_vma=False
    )
```

```python
import functools
import math

import jax
import jax.numpy as jnp
import numpy as np
from jax import lax
from jax.experimental import pallas as pl
from jax.experimental.pallas import tpu as pltpu
from jax.sharding import PartitionSpec as P

MESH = pl.DeviceIdType.MESH
FFT = 2048
TAPS = 4
CHANNELS = 32
ROWS = 2 * CHANNELS
HALO = TAPS - 1
CHANS = 16
TILES = 8
RING = 4
FRAMES = 16
PARTS = 2
SPECTRA = FRAMES // PARTS
BLOCK = 2 * SPECTRA
CHUNKS = ((0, 1), (1, 2))
PAUSE = 16
STEP = 2
CH_DEV = CHANNELS // CHANS
INPUTS = 256
LANES = 128
DEPTH = 2 * FRAMES * CHANS
CUT = 9
CUT_A = 5
CUT_B = 12


def dft_rows():
    samples = np.arange(FFT, dtype=np.int64)
    centers = FFT // 8 + np.arange(CHANNELS, dtype=np.int64)
    angle = 2.0 * np.pi / FFT * (centers[:, None] * samples[None, :] % FFT)
    factor = 1.0 / math.sqrt(FFT)
    return np.concatenate([np.cos(angle), -np.sin(angle)], axis=0).astype(np.float32) * np.float32(factor)


def folded(pfb_taps):
    full = pfb_taps[:, None, :] * dft_rows()[None]
    high = lax.reduce_precision(full, 8, 7)
    return high.astype(jnp.bfloat16), (full - high).astype(jnp.bfloat16)


def spread_kernel(
    high_ref,
    low_ref,
    volt_ref,
    spread_ref,
    left_ref,
    frames,
    weights,
    sums,
    ahead,
    outbox,
    own,
    frame_sem,
    halo_send,
    halo_recv,
    turn_send,
    turn_recv,
    self_sem,
    ring_send,
    ring_recv,
    own_sem,
):
    chan = lax.axis_index("chan")
    tile = lax.axis_index("tile")
    row = tile // RING
    col = lax.rem(tile, RING)
    right = row * RING + lax.rem(col + 1, RING)
    left = row * RING + lax.rem(col + 3, RING)
    far = row * RING + lax.rem(col + 2, RING)
    other = (1 - row) * RING
    across = other + col
    across_right = other + lax.rem(col + 1, RING)
    across_left = other + lax.rem(col + 3, RING)
    across_far = other + lax.rem(col + 2, RING)

    def frame_copy(f):
        return pltpu.make_async_copy(volt_ref.at[pl.ds(f * FFT, FFT)], frames.at[f], frame_sem.at[f])

    @pl.loop(0, FRAMES)
    def _(f):
        frame_copy(f).start()

    barrier = pltpu.get_barrier_semaphore()

    @pl.loop(1, CHANS)
    def _(j):
        pl.semaphore_signal(barrier, inc=1, device_id=(lax.rem(chan + j, CHANS), tile), device_id_type=MESH)

    for peer in (right, left, across):
        pl.semaphore_signal(barrier, inc=1, device_id=(chan, peer), device_id_type=MESH)

    for t in range(TAPS):
        weights[t * ROWS : (t + 1) * ROWS, :] = high_ref[t]
        weights[(TAPS + t) * ROWS : (TAPS + t + 1) * ROWS, :] = low_ref[t]
    sums[:, 0 : HALO * ROWS, :] = jnp.zeros((INPUTS // LANES, HALO * ROWS, LANES), jnp.float32)

    def add_frame(part, f):
        for t in range(TAPS):
            term = part[t * ROWS : (t + 1) * ROWS] + part[(TAPS + t) * ROWS : (TAPS + t + 1) * ROWS]
            at = pl.ds(pl.multiple_of((f + HALO - t) * ROWS, ROWS), ROWS)
            for lane in range(INPUTS // LANES):
                here = term[:, lane * LANES : (lane + 1) * LANES]
                if t == 0:
                    sums[lane, at, :] = here
                else:
                    sums[lane, at, :] += here

    def channelize(start, stop):
        @pl.loop(0, (stop - start) // 2)
        def _(g):
            f = start + 2 * g
            frame_copy(f).wait()
            frame_copy(f + 1).wait()
            pair = jnp.concatenate([frames[f], frames[f + 1]], axis=1)
            part = jnp.dot(weights[...], pair, preferred_element_type=jnp.float32)
            add_frame(part[:, :INPUTS], f)
            add_frame(part[:, INPUTS:], f + 1)

        if (stop - start) % 2:
            frame_copy(stop - 1).wait()
            add_frame(jnp.dot(weights[...], frames[stop - 1], preferred_element_type=jnp.float32), stop - 1)

    def turn(h, j, arriving):
        peer = lax.rem(chan + j, CHANS)
        return pltpu.make_async_remote_copy(
            src_ref=outbox.at[h, peer],
            dst_ref=spread_ref.at[tile, h * CHANS + (peer if arriving else chan)],
            send_sem=turn_send.at[h, peer],
            recv_sem=turn_recv.at[h, peer if arriving else chan],
            device_id=(peer, tile),
            device_id_type=MESH,
        )

    def kept(h):
        return pltpu.make_async_copy(
            outbox.at[h, chan], spread_ref.at[tile, h * CHANS + chan], self_sem.at[h]
        )

    def send_turn(h):
        @pl.loop(0, CHANS)
        def _(p):
            for c in range(CH_DEV):
                for part in range(*CHUNKS[h]):
                    base = (HALO + part * SPECTRA) * ROWS + p * CH_DEV + c
                    for lane in range(INPUTS // LANES):
                        real = sums[lane, pl.ds(base, SPECTRA, stride=ROWS), :]
                        imag = sums[lane, pl.ds(base + CHANNELS, SPECTRA, stride=ROWS), :]
                        both = jnp.concatenate([real, imag], axis=0).astype(jnp.bfloat16)
                        outbox[part, p, c, :, lane * LANES : (lane + 1) * LANES] = both

        @pl.loop(1, CHANS)
        def _(j):
            turn(h, j, False).start()

        kept(h).start()

    def wait_turn(h):
        @pl.loop(1, CHANS)
        def _(j):
            turn(h, j, True).wait_recv()

        kept(h).wait()

    part_a, part_b = (0, CUT), (CUT, CHANS)
    a_one, a_two = (0, CUT_A), (CUT_A, CUT)
    b_one, b_two = (CUT, CUT_B), (CUT_B, CHANS)
    kinds = (
        (right, tile, left, part_a),
        (right, tile, left, part_b),
        (right, across, across_left, part_a),
        (right, left, far, a_one),
        (right, left, far, b_one),
        (right, across_left, across_far, a_one),
        (left, tile, right, part_a),
        (left, tile, right, part_b),
        (left, across, across_right, part_a),
        (left, right, far, a_two),
        (left, right, far, b_two),
        (left, across_right, across_far, a_two),
        (across, tile, across, part_a),
        (across, tile, across, part_b),
        (across, left, across_left, part_b),
        (across, right, across_right, part_b),
        (across, far, across_far, b_one),
        (across, far, across_far, b_two),
    )

    def message(h, kind, arriving):
        to, sent, received, pieces = kinds[kind]
        slot = received if arriving else sent
        block = spread_ref.at[slot, pl.ds(h * CHANS + pieces[0], pieces[1] - pieces[0])]
        return pltpu.make_async_remote_copy(
            src_ref=block,
            dst_ref=block,
            send_sem=ring_send.at[h, kind],
            recv_sem=ring_recv.at[h, kind],
            device_id=(chan, to),
            device_id_type=MESH,
        )

    def send(h, *which):
        for kind in which:
            message(h, kind, False).start()

    def wait(h, *which):
        for kind in which:
            message(h, kind, True).wait_recv()

    def open_ring(h):
        wait_turn(h)
        send(h, 12, 1, 7, 0, 6, 13)

    def first_hops(h):
        wait(h, 12)
        send(h, 2, 8)
        wait(h, 1)
        send(h, 4, 14)
        wait(h, 7)
        send(h, 10, 15)

    def last_hops(h):
        wait(h, 0)
        send(h, 3)
        wait(h, 6)
        send(h, 9)
        wait(h, 4)
        send(h, 16)
        wait(h, 10)
        send(h, 17)
        wait(h, 2)
        send(h, 5)
        wait(h, 8)
        send(h, 11)

    channelize(0, HALO + 1)
    pl.semaphore_wait(barrier, CHANS - 1 + 3)
    behind = pltpu.make_async_remote_copy(
        src_ref=sums.at[:, pl.ds(0, HALO * ROWS)],
        dst_ref=ahead,
        send_sem=halo_send,
        recv_sem=halo_recv,
        device_id=(lax.rem(chan + CHANS - 1, CHANS), tile),
        device_id_type=MESH,
    )
    behind.start()
    ready = [last * SPECTRA + HALO for _, last in CHUNKS[:-1]]
    channelize(HALO + 1, ready[0])
    send_turn(0)
    channelize(ready[0], PAUSE)
    open_ring(0)
    channelize(PAUSE, FRAMES)
    behind.wait()
    ending = pl.ds(FRAMES * ROWS, HALO * ROWS)
    sums[:, ending, :] += jnp.where(chan == CHANS - 1, 0.0, ahead[...])
    send_turn(1)
    first_hops(0)
    open_ring(1)
    fetch = pltpu.make_async_copy(spread_ref.at[tile], own, own_sem)
    fetch.start()
    last_hops(0)
    fetch.wait()

    def prepare(c):
        mine = own[:, c].astype(jnp.float32).reshape(DEPTH, INPUTS).T
        at = lax.broadcasted_iota(jnp.int32, mine.shape, 1)
        upper = lax.rem(at, BLOCK) < SPECTRA
        swapped = jnp.where(upper, jnp.roll(mine, -SPECTRA, axis=1), -jnp.roll(mine, SPECTRA, axis=1))
        left_ref[c, 0:INPUTS, :] = mine.astype(jnp.bfloat16)
        left_ref[c, INPUTS : 2 * INPUTS, :] = swapped.astype(jnp.bfloat16)

    prepare(0)
    first_hops(1)
    prepare(1)
    last_hops(1)
    for h in range(len(CHUNKS)):
        wait(h, 3, 9, 5, 11, 13, 14, 15, 16, 17)
    for h in range(len(CHUNKS)):
        for kind in range(len(kinds)):
            message(h, kind, False).wait_send()

        @pl.loop(1, CHANS)
        def _(j):
            turn(h, j, False).wait_send()


def spread(high, low, voltages):
    kinds = 18
    chunks = len(CHUNKS)
    vmem = pl.BlockSpec(memory_space=pltpu.VMEM)
    hbm = pl.BlockSpec(memory_space=pltpu.HBM)
    dma = pltpu.SemaphoreType.DMA
    return pl.pallas_call(
        spread_kernel,
        in_specs=[vmem, vmem, hbm],
        out_specs=[vmem, vmem],
        out_shape=[
            jax.ShapeDtypeStruct((TILES, PARTS * CHANS, CH_DEV, BLOCK, INPUTS), jnp.bfloat16),
            jax.ShapeDtypeStruct((CH_DEV, 2 * INPUTS, DEPTH), jnp.bfloat16),
        ],
        scratch_shapes=[
            pltpu.VMEM((FRAMES, FFT, INPUTS), jnp.bfloat16),
            pltpu.VMEM((2 * TAPS * ROWS, FFT), jnp.bfloat16),
            pltpu.VMEM((INPUTS // LANES, (FRAMES + HALO) * ROWS, LANES), jnp.float32),
            pltpu.VMEM((INPUTS // LANES, HALO * ROWS, LANES), jnp.float32),
            pltpu.VMEM((PARTS, CHANS, CH_DEV, BLOCK, INPUTS), jnp.bfloat16),
            pltpu.VMEM((PARTS * CHANS, CH_DEV, BLOCK, INPUTS), jnp.bfloat16),
            dma((FRAMES,)),
            dma,
            dma,
            dma((chunks, CHANS)),
            dma((chunks, CHANS)),
            dma((chunks,)),
            dma((chunks, kinds)),
            dma((chunks, kinds)),
            dma,
        ],
        compiler_params=pltpu.CompilerParams(
            collective_id=0, has_side_effects=True, vmem_limit_bytes=44 << 20
        ),
    )(high, low, voltages)


def correlate_kernel(scale, left_ref, other_ref, out_ref, planes, sems):
    copies = []
    for c in range(CH_DEV):
        for q in range(TILES):
            right = other_ref[q, :, c].reshape(DEPTH, INPUTS)
            block = jnp.dot(left_ref[c], right, preferred_element_type=jnp.float32) * scale
            planes[c, 0, :, q * INPUTS : (q + 1) * INPUTS] = block[:INPUTS]
            planes[c, 1, :, q * INPUTS : (q + 1) * INPUTS] = block[INPUTS:]
            if (q + 1) % STEP == 0:
                columns = pl.ds((q + 1 - STEP) * INPUTS, STEP * INPUTS)
                copies.append(
                    pltpu.make_async_copy(
                        planes.at[c, :, :, columns], out_ref.at[c, :, :, columns], sems.at[len(copies)]
                    )
                )
                copies[-1].start()
    for copy in copies:
        copy.wait()


def correlate(left, gathered):
    vmem = pl.BlockSpec(memory_space=pltpu.VMEM)
    shape = (CH_DEV, 2, INPUTS, TILES * INPUTS)
    return pl.pallas_call(
        functools.partial(correlate_kernel, 1.0 / (CHANS * FRAMES)),
        in_specs=[vmem, vmem],
        out_specs=pl.BlockSpec(memory_space=pltpu.HBM),
        out_shape=jax.ShapeDtypeStruct(shape, jnp.float32),
        scratch_shapes=[
            pltpu.VMEM(shape, jnp.float32),
            pltpu.SemaphoreType.DMA((CH_DEV * TILES // STEP,)),
        ],
        compiler_params=pltpu.CompilerParams(vmem_limit_bytes=16 << 20),
    )(left, gathered)


def shards(voltages, pfb_taps):
    gathered, left = spread(*folded(pfb_taps), voltages)
    return correlate(left, gathered)


def solution(mesh):
    placed = (P("chan", "tile"), P())
    return jax.shard_map(
        shards, mesh=mesh, in_specs=placed, out_specs=P("chan", None, "tile", None), check_vma=False
    )
```
